32 devices in a mesh: phase: 4 (over x, core), seq: 4 (over z), mp: 2 (over y).
Axes of the slice: x: 2, y: 2, z: 4, core: 2. Of those that a mesh axis runs over, the one named last changes fastest.
Arguments:
- queries: bfloat16 [4, 2048, 4096], P('phase', 'seq', 'mp'), may hold values from -360 to 360
- key_weight: bfloat16 [4, 1024, 4096], P('phase', None, 'mp'), may hold values from -0.1875 to 0.1875
- value_weight: bfloat16 [4, 1024, 4096], P('phase', None, 'mp'), may hold values from -0.1875 to 0.1875
- enc_gain: float32 [1024], replicated, may hold values from 0.25 to 2
- neighbour_states: bfloat16 [80, 64, 1024], P('seq', ('phase', 'mp')), may hold values from -600 to 600
- slot_dest: int32 [80], P('seq'), may hold values from -1 to 63, as said below
Outputs:
- context: bfloat16 [4, 2048, 4096], P('phase', 'seq', 'mp')
The draws below stay inside these ranges and needn't reach their ends.
Inputs may be any that keep to these rules, and one draw needn't show every extreme that they name: slot_dest names every position 0 to 63 exactly once and is -1 elsewhere. Positions 2 * 8 j to 2 * 8 (j + 1) - 1 belong to the tokens of index j of seq. The slots of one index of seq name at most 5 positions of any one index of seq, and this bound is reached; one index of seq has up to 20 filled slots, reached in every draw.
All inputs are finite; a program needn't handle non-finite values.
Results may differ from the reference program's by a relative error of at most 0.0074.
Values may be sent and summed in bfloat16 or wider, within the bound.
No kernel may reach another device: no remote copies, remote signals or barrier semaphores. Data moves between devices by JAX's collectives and lax.ppermute only.
A program may use at most 64 MiB of HBM per device.

```python
import math
import jax
import jax.numpy as jnp
from jax import lax

DE = 1024
HEADS = 32
HD = 128
SEGLEN = 64
NLEN = 64
NEIGH = 2
HQ = 4096
CH_DEV = 8
PHASES = 4
SHARDS = 4
TOKENS = 2048
SEQLEN = 2048
NB_DEV = 20
SLOTS = 80


def draw_queries(key, part):
    base = jnp.clip(jax.random.normal(key, (PHASES, TOKENS, HQ), jnp.float32), -6.0, 6.0)
    return base.astype(jnp.bfloat16)


def draw_neighbour_states(key, part):
    keys = jax.random.split(jax.random.fold_in(key, 11), 3)
    base = jnp.clip(jax.random.normal(keys[0], (SLOTS, NLEN, DE), jnp.float32), -6.0, 6.0)
    column = jnp.exp(jax.random.uniform(keys[1], (DE,), jnp.float32, 0.0, math.log(10.0)))
    rowscale = jnp.exp(jax.random.uniform(keys[2], (SLOTS, NLEN, 1), jnp.float32, 0.0, math.log(10.0)))
    return (base * column * rowscale).astype(jnp.bfloat16)


def draw_slot_dest(key, part):
    count = SHARDS
    per_shard = NEIGH * CH_DEV
    slots_here = NB_DEV
    baseline = per_shard // count
    keys = jax.random.split(jax.random.fold_in(key, 23), 5)
    order = jax.random.permutation(keys[0], count)
    takers = order[0::2]
    givers = order[1::2]
    amount = jax.random.randint(keys[1], (count // 2,), 0, count + 1).at[0].set(count)
    column_perm = jax.vmap(lambda single: jax.random.permutation(single, count))(jax.random.split(keys[2], count // 2))
    column_rank = jnp.argsort(column_perm, axis=1)
    moved = (column_rank < amount[:, None]).astype(jnp.int32)
    senders = jnp.arange(count)
    taker_hot = (takers[:, None] == senders[None, :]).astype(jnp.int32)
    giver_hot = (givers[:, None] == senders[None, :]).astype(jnp.int32)
    counts = baseline + jnp.dot(taker_hot.T, moved) - jnp.dot(giver_hot.T, moved)
    filled = jnp.sum(counts, axis=1)
    running = jnp.cumsum(counts, axis=1)
    slot_index = jnp.arange(slots_here)
    receiver = jnp.sum((running[:, None, :] <= slot_index[None, :, None]).astype(jnp.int32), axis=2)
    is_live = slot_index[None, :] < filled[:, None]
    receiver = jnp.minimum(receiver, count - 1)
    pair_start = jnp.take_along_axis(running - counts, receiver, axis=1)
    slot_rank = slot_index[None, :] - pair_start
    column_start = jnp.cumsum(counts, axis=0) - counts
    first_place = jnp.take_along_axis(column_start, receiver, axis=1) + slot_rank
    receiver_perm = jax.vmap(lambda single: jax.random.permutation(single, per_shard))(jax.random.split(keys[3], count))
    place = receiver_perm[receiver, jnp.clip(first_place, 0, per_shard - 1)]
    dest = jnp.where(is_live, receiver * per_shard + place, -1)
    slot_perm = jax.vmap(lambda single: jax.random.permutation(single, slots_here))(jax.random.split(keys[4], count))
    dest = jnp.take_along_axis(dest, slot_perm, axis=1)
    return dest.reshape(count * slots_here).astype(jnp.int32)


def level_of(stream_key, dims, shards, smallest, top_value):
    gain, own = 1.0, jax.random.fold_in(stream_key, 6)
    for dim, parts in shards:
        draws = jnp.exp(jax.random.uniform(jax.random.fold_in(own, dim), (parts,), jnp.float32, smallest / len(shards), top_value / len(shards)))
        gain = gain * jnp.repeat(draws, dims[dim] // parts).reshape([-1 if axis == dim else 1 for axis in range(len(dims))])
    return gain


def normal_values(stream_key, dims, deviation, bound, pieces=(), dtype=jnp.bfloat16):
    values = jax.random.normal(stream_key, dims, jnp.float32) * deviation
    if len(pieces) > 0:
        values = level_of(stream_key, dims, pieces, -0.22, 0.18) * values
    return jnp.clip(values, min=-bound, max=bound).astype(dtype)


def setup_inputs(seed: int = 0) -> dict:
    splits = jax.random.split(jax.random.key(seed), 7)
    return {
        "queries": draw_queries(jax.random.fold_in(splits[6], 71), 0),
        "key_weight": normal_values(splits[1], (PHASES, DE, HQ), DE ** -0.5, 0.1875, ((0, 4), (2, 2))),
        "value_weight": normal_values(splits[2], (PHASES, DE, HQ), DE ** -0.5, 0.1875, ((0, 4), (2, 2))),
        "enc_gain": jnp.clip(jax.random.uniform(splits[3], (DE,), jnp.float32, 0.25, 2.0), 0.25, 2.0),
        "neighbour_states": draw_neighbour_states(jax.random.fold_in(splits[6], 71), 0),
        "slot_dest": draw_slot_dest(jax.random.fold_in(splits[6], 71), 0),
    }


def reference(queries, key_weight, value_weight, enc_gain, neighbour_states, slot_dest):
    positions = NEIGH * CH_DEV * SHARDS
    states = neighbour_states.astype(jnp.float32)
    meansq = lax.optimization_barrier(jnp.mean(states * states, axis=-1, keepdims=True))
    normed = (states * lax.rsqrt(meansq + 1e-06) * enc_gain.astype(jnp.float32)).astype(jnp.bfloat16)
    target = jnp.where(slot_dest >= 0, slot_dest, positions).astype(jnp.int32)
    neighbours = jnp.zeros((positions + 1, NLEN, DE), jnp.bfloat16).at[target].set(normed)[:positions]
    sequences = TOKENS // SEQLEN
    per_seq = SEQLEN // SEGLEN
    flattened = neighbours.reshape(positions * NLEN, DE)

    def one_phase(operands):
        query_rows, key_mat, value_mat = operands
        keys = jnp.dot(flattened, key_mat, preferred_element_type=jnp.float32).astype(jnp.bfloat16)
        vals = jnp.dot(flattened, value_mat, preferred_element_type=jnp.float32).astype(jnp.bfloat16)
        keys = keys.reshape(sequences, per_seq, NEIGH * NLEN, HQ)
        vals = vals.reshape(sequences, per_seq, NEIGH * NLEN, HQ)
        empty_block = jnp.zeros((sequences, 1, NEIGH * NLEN, HQ), jnp.bfloat16)
        all_keys = jnp.concatenate([empty_block, keys], axis=1).reshape(sequences, per_seq + 1, NEIGH * NLEN, HEADS, HD)
        all_vals = jnp.concatenate([empty_block, vals], axis=1).reshape(sequences, per_seq + 1, NEIGH * NLEN, HEADS, HD)
        seq_rows = query_rows.reshape(sequences, SEQLEN, HQ)
        padded = jnp.concatenate([jnp.zeros((sequences, 1, HQ), jnp.bfloat16), seq_rows, jnp.zeros((sequences, SEGLEN - 1, HQ), jnp.bfloat16)], axis=1)
        padded = padded.reshape(sequences, per_seq + 1, SEGLEN, HEADS, HD)
        scores = jnp.einsum('swqhd,swkhd->swhqk', padded.astype(jnp.float32), all_keys.astype(jnp.float32), precision=lax.Precision.HIGHEST) * HD ** (-0.5)
        top = lax.optimization_barrier(jnp.max(scores, axis=-1, keepdims=True))
        exponent = jnp.exp(scores - top)
        weights = (exponent / lax.optimization_barrier(jnp.sum(exponent, axis=-1, keepdims=True))).astype(jnp.bfloat16)
        context = jnp.einsum('swhqk,swkhd->swqhd', weights.astype(jnp.float32), all_vals.astype(jnp.float32), precision=lax.Precision.HIGHEST)
        context = context.astype(jnp.bfloat16).reshape(sequences, (per_seq + 1) * SEGLEN, HQ)[:, 1:SEQLEN + 1]
        keep = jnp.arange(SEQLEN) >= SEGLEN - 1
        context = jnp.where(keep[None, :, None], context, jnp.zeros_like(context))
        return context.reshape(TOKENS, HQ)
    return lax.map(one_phase, (queries, key_weight, value_weight))
```

```python
import functools
import math

import jax
import jax.numpy as jnp
from jax import lax
from jax.experimental import pallas as pl
from jax.experimental.pallas import tpu as pltpu
from jax.sharding import PartitionSpec as P


HD = 128
SEGLEN = 64
NEIGH = 2
LANES = 128
TILE = 8
EDGE = 16
FAR = 255.0
VMEM_LIMIT = 18 << 20
LAGS = (15, 30, 31)


def normalize(rows, gain):
    states = rows.astype(jnp.float32)
    meansq = jnp.mean(states * states, axis=-1, keepdims=True)
    return (states * lax.rsqrt(meansq + 1e-06) * gain).astype(jnp.bfloat16)


def pack_kernel(dest_hbm, place_ref, rows_hbm, gain_hbm, *refs, per_shard, capacity):
    parcels = refs[:-6]
    held, normed, dest_ref, rows_ref, gain_ref, sems = refs[-6:]
    shards = len(parcels)
    slots, tall, depth = rows_ref.shape
    feats = depth // LANES
    span = capacity * tall
    copies = [
        pltpu.make_async_copy(source, target, sems.at[index])
        for index, (source, target) in enumerate(
            ((rows_hbm, rows_ref), (gain_hbm, gain_ref), (dest_hbm, dest_ref))
        )
    ]
    for copy in copies:
        copy.start()
    held[...] = jnp.zeros_like(held)
    for copy in copies:
        copy.wait()
    normed[...] = normalize(rows_ref[...], gain_ref[...])
    lane = lax.broadcasted_iota(jnp.int32, (TILE, LANES), 1)
    counts = [jnp.int32(0)] * shards
    targets = [jnp.full((TILE, LANES), FAR, jnp.float32) for _ in range(shards)]
    for slot in range(slots):
        dest = dest_ref[slot]
        live = dest >= 0
        shard = jnp.where(live, dest, 0) // per_shard
        away = lax.rem(shard - place_ref[0] + shards, shards)
        away = jnp.where(live, away, shards)
        rank = jnp.int32(0)
        for other in range(shards):
            hit = away == other
            rank = jnp.where(hit, counts[other], rank)
            counts[other] = counts[other] + hit.astype(jnp.int32)
        index = away * capacity + rank
        for feat in range(feats):
            cols = slice(feat * LANES, (feat + 1) * LANES)
            held[index, feat * tall : (feat + 1) * tall, :] = normed[slot, :, cols]
        begin = rank * tall
        inside = (lane >= begin) & (lane < begin + tall)
        row = ((dest - shard * per_shard) * tall - begin + lane).astype(jnp.float32)
        for other in range(shards):
            targets[other] = jnp.where(inside & (away == other), row, targets[other])
    for shard in range(shards):
        for rank in range(capacity):
            begin = rank * feats * tall
            parcels[shard][begin : begin + feats * tall, :] = held[shard * capacity + rank]
        parcels[shard][feats * span :, :] = targets[shard].astype(jnp.bfloat16)


def pack(slot_dest, own, rows, gain, shards, per_shard, capacity):
    _, tall, depth = rows.shape
    size = depth // LANES * capacity * tall
    parcel = jax.ShapeDtypeStruct((size + TILE, LANES), jnp.bfloat16)
    return pl.pallas_call(
        functools.partial(pack_kernel, per_shard=per_shard, capacity=capacity),
        out_shape=[parcel] * shards,
        in_specs=[
            pl.BlockSpec(memory_space=pltpu.HBM),
            pl.BlockSpec(memory_space=pltpu.SMEM),
            pl.BlockSpec(memory_space=pltpu.HBM),
            pl.BlockSpec(memory_space=pltpu.HBM),
        ],
        out_specs=[pl.BlockSpec(memory_space=pltpu.VMEM)] * shards,
        scratch_shapes=[
            pltpu.VMEM((shards * capacity + 1, size // capacity, LANES), jnp.bfloat16),
            pltpu.VMEM(rows.shape, jnp.bfloat16),
            pltpu.SMEM(slot_dest.shape, jnp.int32),
            pltpu.VMEM(rows.shape, jnp.bfloat16),
            pltpu.VMEM((1, depth), jnp.float32),
            pltpu.SemaphoreType.DMA((3,)),
        ],
        compiler_params=pltpu.CompilerParams(vmem_limit_bytes=VMEM_LIMIT),
        name="pack",
    )(
        pltpu.with_memory_space_constraint(slot_dest, pltpu.HBM),
        own,
        pltpu.with_memory_space_constraint(rows, pltpu.HBM),
        pltpu.with_memory_space_constraint(gain.reshape(1, depth), pltpu.HBM),
    )


def unpack_kernel(*refs, tall):
    parcels, (block_ref, tail_ref) = refs[:-2], refs[-2:]
    rows, depth = block_ref.shape
    feats = depth // LANES
    span = (parcels[0].shape[0] - TILE) // feats
    place = lax.broadcasted_iota(jnp.int32, (rows, span), 0).astype(jnp.float32)
    picks = [
        (ref[feats * span :, :][:1, :span].astype(jnp.float32) == place).astype(jnp.bfloat16)
        for ref in parcels
    ]
    tail = tail_ref.shape[0]
    for feat in range(feats):
        total = jnp.zeros((rows, LANES), jnp.float32)
        for pick, ref in zip(picks, parcels):
            starts = range(feat * tall, feats * span, feats * tall)
            arrived = jnp.concatenate([ref[begin : begin + tall, :] for begin in starts], axis=0)
            total = total + jnp.dot(pick, arrived, preferred_element_type=jnp.float32)
        placed = total.astype(jnp.bfloat16)
        block_ref[:, feat * LANES : (feat + 1) * LANES] = placed
        tail_ref[:, feat * LANES : (feat + 1) * LANES] = placed[rows - tail :]


def unpack(parcels, depth, per_shard, tall):
    return pl.pallas_call(
        functools.partial(unpack_kernel, tall=tall),
        out_shape=[
            jax.ShapeDtypeStruct((per_shard * tall, depth), jnp.bfloat16),
            jax.ShapeDtypeStruct((NEIGH * tall, depth), jnp.bfloat16),
        ],
        compiler_params=pltpu.CompilerParams(vmem_limit_bytes=VMEM_LIMIT),
        name="unpack",
    )(*parcels)


def packing(slot_dest, shards, per_shard, capacity):
    count = slot_dest.shape[0]
    is_live = slot_dest >= 0
    target = jnp.where(is_live, slot_dest // per_shard, -1)
    order = jnp.arange(count)
    earlier = (target[:, None] == target[None, :]) & (order[None, :] < order[:, None])
    slot_rank = jnp.sum(earlier.astype(jnp.int32), axis=1)
    buffer_slot = jnp.where(is_live, target * capacity + slot_rank, -1)
    matches = jnp.arange(shards * capacity)[:, None] == buffer_slot[None, :]
    selector = matches.astype(jnp.bfloat16)
    sent_dest = jnp.sum(jnp.where(matches, slot_dest[None, :] + 1, 0), axis=1) - 1
    return selector, sent_dest.reshape(shards, capacity)


def select_rows(selector, rows):
    flattened = rows.reshape(rows.shape[0], -1)
    chosen = jnp.dot(selector, flattened, preferred_element_type=jnp.float32)
    return chosen.astype(jnp.bfloat16).reshape(selector.shape[0], *rows.shape[1:])


def route_plain(slot_dest, normed, own, shards, per_shard, capacity):
    selector, sent_dest = packing(slot_dest, shards, per_shard, capacity)
    sent = select_rows(selector, normed).reshape(shards, capacity, *normed.shape[1:])
    received = lax.all_to_all(sent, "seq", split_axis=0, concat_axis=0, tiled=True)
    received_dest = lax.all_to_all(sent_dest, "seq", split_axis=0, concat_axis=0, tiled=True)
    flat_dest = received_dest.reshape(-1)
    local = jnp.where(flat_dest >= 0, flat_dest - own * per_shard, -1)
    placer = (jnp.arange(per_shard)[:, None] == local[None, :]).astype(jnp.bfloat16)
    return select_rows(placer, received.reshape(shards * capacity, *normed.shape[1:]))


def hold_kernel(*refs):
    half = (len(refs) - 1) // 2
    sems = refs[-1]
    copies = [
        pltpu.make_async_copy(refs[index], refs[half + index], sems.at[index])
        for index in range(half)
    ]
    for copy in copies:
        copy.start()
    for copy in copies:
        copy.wait()


def hold(*arrays):
    return pl.pallas_call(
        hold_kernel,
        out_shape=[jax.ShapeDtypeStruct(array.shape, array.dtype) for array in arrays],
        in_specs=[pl.BlockSpec(memory_space=pltpu.HBM)] * len(arrays),
        out_specs=[pl.BlockSpec(memory_space=pltpu.VMEM)] * len(arrays),
        scratch_shapes=[pltpu.SemaphoreType.DMA((len(arrays),))],
        compiler_params=pltpu.CompilerParams(vmem_limit_bytes=VMEM_LIMIT),
        cost_estimate=pl.CostEstimate(
            flops=0, bytes_accessed=2 * sum(array.nbytes for array in arrays), transcendentals=0
        ),
        name="hold",
    )(*(pltpu.with_memory_space_constraint(array, pltpu.HBM) for array in arrays))


def resident(*arrays):
    return [pltpu.with_memory_space_constraint(array, pltpu.VMEM) for array in arrays]


def project_kernel(*refs, parts, stage, aliased, cols):
    blocks, (wk_ref, wv_ref) = refs[:parts], refs[parts : parts + 2]
    k_ref, v_ref, x_scr = refs[parts + (4 if aliased else 2) :]
    rows = blocks[0].shape[0]
    segs = k_ref.shape[1]
    tall = rows // segs
    base = stage * parts * tall
    for part in range(parts):
        x_scr[part * rows : (part + 1) * rows, :] = blocks[part][...]

    for step in range(wk_ref.shape[2] // cols):
        here = slice(step * cols, (step + 1) * cols)
        for w_ref, ref in ((wk_ref, k_ref), (wv_ref, v_ref)):
            out = jnp.dot(x_scr[...], w_ref[0, :, here], preferred_element_type=jnp.float32)
            out = out.astype(jnp.bfloat16)
            for part in range(parts):
                put = base + part * tall
                for seg in range(segs):
                    start = part * rows + seg * tall
                    for head in range(cols // HD):
                        ref[step * (cols // HD) + head, seg, put : put + tall, :] = out[
                            start : start + tall, head * HD : (head + 1) * HD
                        ]


def project(blocks, key_weight, value_weight, stage, stages, segs, carried=(), cols=512):
    parts = len(blocks)
    rows, depth = blocks[0].shape
    width = key_weight.shape[-1]
    keys = rows * parts // segs
    shape = jax.ShapeDtypeStruct((width // HD, segs, keys * stages, HD), jnp.bfloat16)
    vmem = pl.BlockSpec(memory_space=pltpu.VMEM)
    return pl.pallas_call(
        functools.partial(
            project_kernel, parts=parts, stage=stage, aliased=bool(carried), cols=cols
        ),
        out_shape=[shape, shape],
        in_specs=[vmem] * (parts + 2 + len(carried)),
        out_specs=[vmem, vmem],
        scratch_shapes=[pltpu.VMEM((rows * parts, depth), jnp.bfloat16)],
        input_output_aliases={parts + 2: 0, parts + 3: 1} if carried else {},
        compiler_params=pltpu.CompilerParams(vmem_limit_bytes=VMEM_LIMIT),
        cost_estimate=pl.CostEstimate(
            flops=4 * rows * parts * depth * width, bytes_accessed=0, transcendentals=0
        ),
        name="project",
    )(*blocks, *resident(key_weight, value_weight, *carried))


def attend_kernel(place_ref, *refs, counts, heads):
    mains, befores = counts
    blocks, refs = refs[: mains + befores], refs[mains + befores :]
    wk_ref, wv_ref, q_ref = refs[:3]
    kept = refs[3:-6]
    o_ref, x_scr, k_scr, v_scr, kb_scr, vb_scr = refs[-6:]
    count = k_scr.shape[0]
    rows = blocks[0].shape[0]
    tall = rows // count
    held = kept[0].shape[2] if kept else 0

    @pl.when(pl.program_id(0) == 0)
    def _():
        start = 0
        for ref in blocks:
            x_scr[start : start + ref.shape[0], :] = ref[...]
            start += ref.shape[0]

    width = heads * HD
    here = pl.ds(pl.multiple_of(pl.program_id(0) * width, width), width)
    for w_ref, scr, before_scr in ((wk_ref, k_scr, kb_scr), (wv_ref, v_scr, vb_scr)):
        w = w_ref[0, :, here] if kept else w_ref[0]
        out = jnp.dot(x_scr[...], w, preferred_element_type=jnp.float32)
        out = out.astype(jnp.bfloat16)
        for part in range(mains):
            for seg in range(count):
                start = part * rows + seg * tall
                put = held + part * tall
                scr[seg, put : put + tall, :] = out[start : start + tall]
        before_scr[...] = out[mains * rows :]

    for scr, ref in zip((k_scr, v_scr), kept):
        for head in range(heads):
            for seg in range(count):
                scr[seg, :held, head * HD : (head + 1) * HD] = ref[head, seg]

    def keys_of(which, seg, cols):
        if seg == 0:
            return (kb_scr, vb_scr)[which][:, cols]
        own = (k_scr, v_scr)[which][seg - 1, :, cols]
        return own

    scale = HD ** (-0.5) * math.log2(math.e)
    last = lax.broadcasted_iota(jnp.int32, (EDGE, 1), 0) == EDGE - 1
    whole = lax.broadcasted_iota(jnp.int32, (SEGLEN, 1), 0) == SEGLEN - 1
    heard = whole | (place_ref[1] == 0)

    def split(out, seg):
        return (out[:EDGE] if seg else None), out[EDGE if seg else 0 :]

    def join(outs, unit):
        lead, tail = outs[unit][1], outs[unit + 1][0]
        end = jnp.where(last, tail, lead[SEGLEN - EDGE :])
        return jnp.concatenate([lead[: SEGLEN - EDGE], end], axis=0)

    def score(head, seg):
        begin = SEGLEN * seg - (EDGE if seg else 0)
        end = SEGLEN * seg + (SEGLEN if seg < count else 0)
        out = lax.dot_general(
            q_ref[0, begin:end, head * HD : (head + 1) * HD],
            keys_of(0, seg, slice(head * HD, (head + 1) * HD)),
            (((1,), (1,)), ((), ())),
            preferred_element_type=jnp.float32,
        )
        return split(out, seg)

    def weigh(rows):
        top = jnp.max(rows, axis=-1, keepdims=True)
        exponent = jnp.exp2((rows - top) * scale)
        total = jnp.sum(exponent, axis=-1, keepdims=True)
        return (exponent * (1.0 / total)).astype(jnp.bfloat16)

    def gather(head, seg, unit):
        pieces = []
        if seg:
            pieces.append(weights[unit - 1][SEGLEN - EDGE :])
        if seg < count:
            pieces.append(weights[unit])
        lhs = jnp.concatenate(pieces, axis=0)
        values = keys_of(1, seg, slice(head * HD, (head + 1) * HD))
        return split(jnp.dot(lhs, values, preferred_element_type=jnp.float32), seg)

    units = [(head, seg) for head in range(heads) for seg in range(count + 1)]
    scores, weights, contexts = {}, {}, {}
    for turn in range(len(units) + LAGS[2]):
        if turn < len(units):
            scores[turn] = score(*units[turn])
        unit = turn - LAGS[0]
        if 0 <= unit < len(units) and units[unit][1] < count:
            weights[unit] = weigh(join(scores, unit))
        unit = turn - LAGS[1]
        if 0 <= unit < len(units):
            contexts[unit] = gather(*units[unit], unit)
        unit = turn - LAGS[2]
        if 0 <= unit < len(units) and units[unit][1] < count:
            head, block = units[unit]
            context = join(contexts, unit)
            if block == 0:
                context = jnp.where(heard, context, 0.0)
            span = slice(block * SEGLEN, (block + 1) * SEGLEN)
            o_ref[0, span, head * HD : (head + 1) * HD] = context.astype(jnp.bfloat16)


def attend(place, blocks, before, key_weight, value_weight, queries, kept=(), heads=4):
    depth = before[0].shape[1]
    _, tokens, width = queries.shape
    count = tokens // SEGLEN
    total = sum(block.shape[0] for block in blocks)
    halo = sum(block.shape[0] for block in before)
    cols = heads * HD
    column = lambda i, place: (0, 0, i)
    if kept:
        key_weight, value_weight, *kept = resident(key_weight, value_weight, *kept)
    held = kept[0].shape[2] if kept else 0
    late = pltpu.VMEM((count, held + total // count, cols), jnp.bfloat16)
    past = pltpu.VMEM((halo, cols), jnp.bfloat16)
    return pl.pallas_call(
        functools.partial(attend_kernel, counts=(len(blocks), len(before)), heads=heads),
        out_shape=jax.ShapeDtypeStruct(queries.shape, jnp.bfloat16),
        grid_spec=pltpu.PrefetchScalarGridSpec(
            num_scalar_prefetch=1,
            grid=(width // cols,),
            in_specs=[
                pl.BlockSpec(rows.shape, lambda i, place: (0, 0), pipeline_mode=pl.Buffered(1))
                for rows in (*blocks, *before)
            ]
            + [pl.BlockSpec(memory_space=pltpu.VMEM) if kept else pl.BlockSpec((1, depth, cols), column)] * 2
            + [pl.BlockSpec((1, tokens, cols), column)]
            + [
                pl.BlockSpec((heads, *rows.shape[1:]), lambda i, place: (i, 0, 0, 0))
                for rows in kept
            ],
            out_specs=pl.BlockSpec((1, tokens, cols), column),
            scratch_shapes=[
                pltpu.VMEM((total + halo, depth), jnp.bfloat16),
                late,
                late,
                past,
                past,
            ],
        ),
        compiler_params=pltpu.CompilerParams(
            dimension_semantics=("arbitrary",), vmem_limit_bytes=VMEM_LIMIT
        ),
        name="attend",
    )(place, *blocks, *before, key_weight, value_weight, queries, *kept)


def swap(rows, axes, sizes, move):
    pairs = []
    for phase in range(sizes[0]):
        for part in range(sizes[1]):
            to = move(phase, part)
            pairs.append((phase * sizes[1] + part, to[0] * sizes[1] + to[1]))
    return lax.ppermute(rows, axes, pairs)


def on_device_staged(place, block, tail, ahead, sizes, key_weight, value_weight, queries):
    axes = ("phase", "mp")
    core = lambda rows: swap(rows, axes, sizes, lambda p, m: (p ^ 1, m))
    x_even = lambda rows: swap(
        rows, axes, sizes, lambda p, m: (p ^ 2, m) if p % 2 == 0 else (p, m ^ 1)
    )
    y_even = lambda rows: swap(
        rows, axes, sizes, lambda p, m: (p ^ 2, m) if p % 2 else (p, m ^ 1)
    )
    segs = queries.shape[1] // SEGLEN

    over_a = y_even(block)
    over_b = x_even(block)
    beside = core(block)
    passed = lax.ppermute(tail, "seq", ahead)
    carried = project([block, beside], key_weight, value_weight, 0, 4, segs)
    corner = x_even(over_a)
    beside_a = core(over_a)
    beside_b = core(over_b)
    passed = jnp.concatenate([passed, y_even(passed)], axis=0)
    carried = project([over_a, over_b], key_weight, value_weight, 1, 4, segs, carried)
    passed = jnp.concatenate([passed, x_even(passed)], axis=0)
    before = core(passed)
    beside_corner = core(corner)
    carried = project([beside_a, beside_b], key_weight, value_weight, 2, 4, segs, carried)
    carried = project([corner, beside_corner], key_weight, value_weight, 3, 4, segs, carried)
    before = [passed, before]
    return attend(place, [], before, key_weight, value_weight, queries, carried)


def attention(queries, key_weight, value_weight, enc_gain, neighbour_states, slot_dest):
    shards = lax.axis_size("seq")
    sizes = (lax.axis_size("phase"), lax.axis_size("mp"))
    own = lax.axis_index("seq")
    tokens_here = queries.shape[1]
    per_shard = NEIGH * (tokens_here // SEGLEN)
    capacity = per_shard // shards + 1
    _, tall, depth = neighbour_states.shape
    ahead = [(i, i + 1) for i in range(shards - 1)]
    even = lax.axis_index("phase") & 1 ^ 1
    place = jnp.stack([own, jnp.where(own == 0, 1, 0), even]).astype(jnp.int32)
    if sizes == (4, 2) and tall % TILE == 0 and capacity * tall <= LANES:
        parcels = pack(
            slot_dest,
            place,
            neighbour_states,
            enc_gain,
            shards,
            per_shard,
            capacity,
        )
        key_weight, value_weight = hold(key_weight, value_weight)
        arrived = [parcels[0]]
        for away in range(1, shards):
            pairs = [(i, (i + away) % shards) for i in range(shards)]
            arrived.append(lax.ppermute(parcels[away], "seq", pairs))
        block, tail = unpack(arrived, depth, per_shard, tall)
        return on_device_staged(
            place, block, tail, ahead, sizes, key_weight, value_weight, queries
        )
    normed = normalize(neighbour_states, enc_gain)
    block = route_plain(slot_dest, normed, own, shards, per_shard, capacity)
    before = lax.ppermute(block[per_shard - NEIGH :], "seq", ahead)
    block = jnp.concatenate([block, before], axis=0)
    routed = lax.all_gather(block, ("phase", "mp"), axis=1, tiled=True)
    mine, before = routed[:per_shard], routed[per_shard:]
    return attend(
        place,
        [mine.reshape(-1, depth)],
        [before.reshape(-1, depth)],
        key_weight,
        value_weight,
        queries,
    )


def solution(mesh):
    in_specs = (
        P("phase", "seq", "mp"),
        P("phase", None, "mp"),
        P("phase", None, "mp"),
        P(),
        P("seq", ("phase", "mp"), None),
        P("seq"),
    )
    out_specs = P("phase", "seq", "mp")
    return jax.shard_map(
        attention, mesh=mesh, in_specs=in_specs, out_specs=out_specs, check_vma=False
    )
```

```python
import functools
import math

import jax
import jax.numpy as jnp
from jax import lax
from jax.experimental import pallas as pl
from jax.experimental.pallas import tpu as pltpu
from jax.sharding import PartitionSpec as P


HD = 128
SEGLEN = 64
NEIGH = 2
LANES = 128
TILE = 8
EDGE = 16
FAR = 255.0
VMEM_LIMIT = 18 << 20
LAGS = (15, 30, 31)


def normalize(rows, gain):
    states = rows.astype(jnp.float32)
    meansq = jnp.mean(states * states, axis=-1, keepdims=True)
    return (states * lax.rsqrt(meansq + 1e-06) * gain).astype(jnp.bfloat16)


def pack_kernel(dest_hbm, place_ref, rows_hbm, gain_hbm, *refs, per_shard, capacity):
    parcels = refs[:-6]
    held, normed, dest_ref, rows_ref, gain_ref, sems = refs[-6:]
    shards = len(parcels)
    slots, tall, depth = rows_ref.shape
    feats = depth // LANES
    span = capacity * tall
    copies = [
        pltpu.make_async_copy(source, target, sems.at[index])
        for index, (source, target) in enumerate(
            ((rows_hbm, rows_ref), (gain_hbm, gain_ref), (dest_hbm, dest_ref))
        )
    ]
    for copy in copies:
        copy.start()
    held[...] = jnp.zeros_like(held)
    for copy in copies:
        copy.wait()
    normed[...] = normalize(rows_ref[...], gain_ref[...])
    lane = lax.broadcasted_iota(jnp.int32, (TILE, LANES), 1)
    counts = [jnp.int32(0)] * shards
    targets = [jnp.full((TILE, LANES), FAR, jnp.float32) for _ in range(shards)]
    for slot in range(slots):
        dest = dest_ref[slot]
        live = dest >= 0
        shard = jnp.where(live, dest, 0) // per_shard
        away = lax.rem(shard - place_ref[0] + shards, shards)
        away = jnp.where(live, away, shards)
        rank = jnp.int32(0)
        for other in range(shards):
            hit = away == other
            rank = jnp.where(hit, counts[other], rank)
            counts[other] = counts[other] + hit.astype(jnp.int32)
        index = away * capacity + rank
        for feat in range(feats):
            cols = slice(feat * LANES, (feat + 1) * LANES)
            held[index, feat * tall : (feat + 1) * tall, :] = normed[slot, :, cols]
        begin = rank * tall
        inside = (lane >= begin) & (lane < begin + tall)
        row = ((dest - shard * per_shard) * tall - begin + lane).astype(jnp.float32)
        for other in range(shards):
            targets[other] = jnp.where(inside & (away == other), row, targets[other])
    for shard in range(shards):
        for rank in range(capacity):
            begin = rank * feats * tall
            parcels[shard][begin : begin + feats * tall, :] = held[shard * capacity + rank]
        parcels[shard][feats * span :, :] = targets[shard].astype(jnp.bfloat16)


def pack(slot_dest, own, rows, gain, shards, per_shard, capacity):
    _, tall, depth = rows.shape
    size = depth // LANES * capacity * tall
    parcel = jax.ShapeDtypeStruct((size + TILE, LANES), jnp.bfloat16)
    return pl.pallas_call(
        functools.partial(pack_kernel, per_shard=per_shard, capacity=capacity),
        out_shape=[parcel] * shards,
        in_specs=[
            pl.BlockSpec(memory_space=pltpu.HBM),
            pl.BlockSpec(memory_space=pltpu.SMEM),
            pl.BlockSpec(memory_space=pltpu.HBM),
            pl.BlockSpec(memory_space=pltpu.HBM),
        ],
        out_specs=[pl.BlockSpec(memory_space=pltpu.VMEM)] * shards,
        scratch_shapes=[
            pltpu.VMEM((shards * capacity + 1, size // capacity, LANES), jnp.bfloat16),
            pltpu.VMEM(rows.shape, jnp.bfloat16),
            pltpu.SMEM(slot_dest.shape, jnp.int32),
            pltpu.VMEM(rows.shape, jnp.bfloat16),
            pltpu.VMEM((1, depth), jnp.float32),
            pltpu.SemaphoreType.DMA((3,)),
        ],
        compiler_params=pltpu.CompilerParams(vmem_limit_bytes=VMEM_LIMIT),
        name="pack",
    )(
        pltpu.with_memory_space_constraint(slot_dest, pltpu.HBM),
        own,
        pltpu.with_memory_space_constraint(rows, pltpu.HBM),
        pltpu.with_memory_space_constraint(gain.reshape(1, depth), pltpu.HBM),
    )


def unpack_kernel(*refs, tall):
    parcels, (block_ref, tail_ref) = refs[:-2], refs[-2:]
    rows, depth = block_ref.shape
    feats = depth // LANES
    span = (parcels[0].shape[0] - TILE) // feats
    place = lax.broadcasted_iota(jnp.int32, (rows, span), 0).astype(jnp.float32)
    picks = [
        (ref[feats * span :, :][:1, :span].astype(jnp.float32) == place).astype(jnp.bfloat16)
        for ref in parcels
    ]
    tail = tail_ref.shape[0]
    for feat in range(feats):
        total = jnp.zeros((rows, LANES), jnp.float32)
        for pick, ref in zip(picks, parcels):
            starts = range(feat * tall, feats * span, feats * tall)
            arrived = jnp.concatenate([ref[begin : begin + tall, :] for begin in starts], axis=0)
            total = total + jnp.dot(pick, arrived, preferred_element_type=jnp.float32)
        placed = total.astype(jnp.bfloat16)
        block_ref[:, feat * LANES : (feat + 1) * LANES] = placed
        tail_ref[:, feat * LANES : (feat + 1) * LANES] = placed[rows - tail :]


def unpack(parcels, depth, per_shard, tall):
    return pl.pallas_call(
        functools.partial(unpack_kernel, tall=tall),
        out_shape=[
            jax.ShapeDtypeStruct((per_shard * tall, depth), jnp.bfloat16),
            jax.ShapeDtypeStruct((NEIGH * tall, depth), jnp.bfloat16),
        ],
        compiler_params=pltpu.CompilerParams(vmem_limit_bytes=VMEM_LIMIT),
        name="unpack",
    )(*parcels)


def packing(slot_dest, shards, per_shard, capacity):
    count = slot_dest.shape[0]
    is_live = slot_dest >= 0
    target = jnp.where(is_live, slot_dest // per_shard, -1)
    order = jnp.arange(count)
    earlier = (target[:, None] == target[None, :]) & (order[None, :] < order[:, None])
    slot_rank = jnp.sum(earlier.astype(jnp.int32), axis=1)
    buffer_slot = jnp.where(is_live, target * capacity + slot_rank, -1)
    matches = jnp.arange(shards * capacity)[:, None] == buffer_slot[None, :]
    selector = matches.astype(jnp.bfloat16)
    sent_dest = jnp.sum(jnp.where(matches, slot_dest[None, :] + 1, 0), axis=1) - 1
    return selector, sent_dest.reshape(shards, capacity)


def select_rows(selector, rows):
    flattened = rows.reshape(rows.shape[0], -1)
    chosen = jnp.dot(selector, flattened, preferred_element_type=jnp.float32)
    return chosen.astype(jnp.bfloat16).reshape(selector.shape[0], *rows.shape[1:])


def route_plain(slot_dest, normed, own, shards, per_shard, capacity):
    selector, sent_dest = packing(slot_dest, shards, per_shard, capacity)
    sent = select_rows(selector, normed).reshape(shards, capacity, *normed.shape[1:])
    received = lax.all_to_all(sent, "seq", split_axis=0, concat_axis=0, tiled=True)
    received_dest = lax.all_to_all(sent_dest, "seq", split_axis=0, concat_axis=0, tiled=True)
    flat_dest = received_dest.reshape(-1)
    local = jnp.where(flat_dest >= 0, flat_dest - own * per_shard, -1)
    placer = (jnp.arange(per_shard)[:, None] == local[None, :]).astype(jnp.bfloat16)
    return select_rows(placer, received.reshape(shards * capacity, *normed.shape[1:]))


def hold_kernel(*refs):
    half = (len(refs) - 1) // 2
    sems = refs[-1]
    copies = [
        pltpu.make_async_copy(refs[index], refs[half + index], sems.at[index])
        for index in range(half)
    ]
    for copy in copies:
        copy.start()
    for copy in copies:
        copy.wait()


def hold(*arrays):
    return pl.pallas_call(
        hold_kernel,
        out_shape=[jax.ShapeDtypeStruct(array.shape, array.dtype) for array in arrays],
        in_specs=[pl.BlockSpec(memory_space=pltpu.HBM)] * len(arrays),
        out_specs=[pl.BlockSpec(memory_space=pltpu.VMEM)] * len(arrays),
        scratch_shapes=[pltpu.SemaphoreType.DMA((len(arrays),))],
        compiler_params=pltpu.CompilerParams(vmem_limit_bytes=VMEM_LIMIT),
        cost_estimate=pl.CostEstimate(
            flops=0, bytes_accessed=2 * sum(array.nbytes for array in arrays), transcendentals=0
        ),
        name="hold",
    )(*(pltpu.with_memory_space_constraint(array, pltpu.HBM) for array in arrays))


def resident(*arrays):
    return [pltpu.with_memory_space_constraint(array, pltpu.VMEM) for array in arrays]


def project_kernel(*refs, parts, stage, aliased, cols):
    blocks, (wk_ref, wv_ref) = refs[:parts], refs[parts : parts + 2]
    k_ref, v_ref, x_scr = refs[parts + (4 if aliased else 2) :]
    rows = blocks[0].shape[0]
    segs = k_ref.shape[1]
    tall = rows // segs
    base = stage * parts * tall
    for part in range(parts):
        x_scr[part * rows : (part + 1) * rows, :] = blocks[part][...]

    for step in range(wk_ref.shape[2] // cols):
        here = slice(step * cols, (step + 1) * cols)
        for w_ref, ref in ((wk_ref, k_ref), (wv_ref, v_ref)):
            out = jnp.dot(x_scr[...], w_ref[0, :, here], preferred_element_type=jnp.float32)
            out = out.astype(jnp.bfloat16)
            for part in range(parts):
                put = base + part * tall
                for seg in range(segs):
                    start = part * rows + seg * tall
                    for head in range(cols // HD):
                        ref[step * (cols // HD) + head, seg, put : put + tall, :] = out[
                            start : start + tall, head * HD : (head + 1) * HD
                        ]


def project(blocks, key_weight, value_weight, stage, stages, segs, carried=(), cols=512):
    parts = len(blocks)
    rows, depth = blocks[0].shape
    width = key_weight.shape[-1]
    keys = rows * parts // segs
    shape = jax.ShapeDtypeStruct((width // HD, segs, keys * stages, HD), jnp.bfloat16)
    vmem = pl.BlockSpec(memory_space=pltpu.VMEM)
    return pl.pallas_call(
        functools.partial(
            project_kernel, parts=parts, stage=stage, aliased=bool(carried), cols=cols
        ),
        out_shape=[shape, shape],
        in_specs=[vmem] * (parts + 2 + len(carried)),
        out_specs=[vmem, vmem],
        scratch_shapes=[pltpu.VMEM((rows * parts, depth), jnp.bfloat16)],
        input_output_aliases={parts + 2: 0, parts + 3: 1} if carried else {},
        compiler_params=pltpu.CompilerParams(vmem_limit_bytes=VMEM_LIMIT),
        cost_estimate=pl.CostEstimate(
            flops=4 * rows * parts * depth * width, bytes_accessed=0, transcendentals=0
        ),
        name="project",
    )(*blocks, *resident(key_weight, value_weight, *carried))


def attend_kernel(place_ref, *refs, counts, heads):
    mains, befores = counts
    blocks, refs = refs[: mains + befores], refs[mains + befores :]
    wk_ref, wv_ref, q_ref = refs[:3]
    kept = refs[3:-6]
    o_ref, x_scr, k_scr, v_scr, kb_scr, vb_scr = refs[-6:]
    count = k_scr.shape[0]
    rows = blocks[0].shape[0]
    tall = rows // count
    held = kept[0].shape[2] if kept else 0

    @pl.when(pl.program_id(0) == 0)
    def _():
        start = 0
        for ref in blocks:
            x_scr[start : start + ref.shape[0], :] = ref[...]
            start += ref.shape[0]

    width = heads * HD
    here = pl.ds(pl.multiple_of(pl.program_id(0) * width, width), width)
    for w_ref, scr, before_scr in ((wk_ref, k_scr, kb_scr), (wv_ref, v_scr, vb_scr)):
        w = w_ref[0, :, here] if kept else w_ref[0]
        out = jnp.dot(x_scr[...], w, preferred_element_type=jnp.float32)
        out = out.astype(jnp.bfloat16)
        for part in range(mains):
            for seg in range(count):
                start = part * rows + seg * tall
                put = held + part * tall
                scr[seg, put : put + tall, :] = out[start : start + tall]
        before_scr[...] = out[mains * rows :]

    def settle(which, head, seg):
        if kept and seg:
            scr = (k_scr, v_scr)[which]
            scr[seg - 1, :held, head * HD : (head + 1) * HD] = kept[which][head, seg - 1]

    def keys_of(which, seg, cols):
        if seg == 0:
            return (kb_scr, vb_scr)[which][:, cols]
        own = (k_scr, v_scr)[which][seg - 1, :, cols]
        return own

    scale = HD ** (-0.5) * math.log2(math.e)
    last = lax.broadcasted_iota(jnp.int32, (EDGE, 1), 0) == EDGE - 1
    whole = lax.broadcasted_iota(jnp.int32, (SEGLEN, 1), 0) == SEGLEN - 1
    heard = whole | (place_ref[1] == 0)

    def split(out, seg):
        return (out[:EDGE] if seg else None), out[EDGE if seg else 0 :]

    def join(outs, unit):
        lead, tail = outs[unit][1], outs[unit + 1][0]
        end = jnp.where(last, tail, lead[SEGLEN - EDGE :])
        return jnp.concatenate([lead[: SEGLEN - EDGE], end], axis=0)

    def score(head, seg):
        begin = SEGLEN * seg - (EDGE if seg else 0)
        end = SEGLEN * seg + (SEGLEN if seg < count else 0)
        out = lax.dot_general(
            q_ref[0, begin:end, head * HD : (head + 1) * HD],
            keys_of(0, seg, slice(head * HD, (head + 1) * HD)),
            (((1,), (1,)), ((), ())),
            preferred_element_type=jnp.float32,
        )
        return split(out, seg)

    def weigh(rows):
        top = jnp.max(rows, axis=-1, keepdims=True)
        exponent = jnp.exp2((rows - top) * scale)
        total = jnp.sum(exponent, axis=-1, keepdims=True)
        return (exponent * (1.0 / total)).astype(jnp.bfloat16)

    def gather(head, seg, unit):
        pieces = []
        if seg:
            pieces.append(weights[unit - 1][SEGLEN - EDGE :])
        if seg < count:
            pieces.append(weights[unit])
        lhs = jnp.concatenate(pieces, axis=0)
        values = keys_of(1, seg, slice(head * HD, (head + 1) * HD))
        return split(jnp.dot(lhs, values, preferred_element_type=jnp.float32), seg)

    units = [(head, seg) for head in range(heads) for seg in range(count + 1)]
    scores, weights, contexts = {}, {}, {}
    for turn in range(len(units) + LAGS[2]):
        if turn < len(units):
            settle(0, *units[turn])
            scores[turn] = score(*units[turn])
        unit = turn - LAGS[0]
        if 0 <= unit < len(units) and units[unit][1] < count:
            weights[unit] = weigh(join(scores, unit))
        unit = turn - LAGS[1]
        if 0 <= unit < len(units):
            settle(1, *units[unit])
            contexts[unit] = gather(*units[unit], unit)
        unit = turn - LAGS[2]
        if 0 <= unit < len(units) and units[unit][1] < count:
            head, block = units[unit]
            context = join(contexts, unit)
            if block == 0:
                context = jnp.where(heard, context, 0.0)
            span = slice(block * SEGLEN, (block + 1) * SEGLEN)
            o_ref[0, span, head * HD : (head + 1) * HD] = context.astype(jnp.bfloat16)


def attend(place, blocks, before, key_weight, value_weight, queries, kept=(), heads=4):
    depth = before[0].shape[1]
    _, tokens, width = queries.shape
    count = tokens // SEGLEN
    total = sum(block.shape[0] for block in blocks)
    halo = sum(block.shape[0] for block in before)
    cols = heads * HD
    column = lambda i, place: (0, 0, i)
    if kept:
        key_weight, value_weight, *kept = resident(key_weight, value_weight, *kept)
    held = kept[0].shape[2] if kept else 0
    late = pltpu.VMEM((count, held + total // count, cols), jnp.bfloat16)
    past = pltpu.VMEM((halo, cols), jnp.bfloat16)
    return pl.pallas_call(
        functools.partial(attend_kernel, counts=(len(blocks), len(before)), heads=heads),
        out_shape=jax.ShapeDtypeStruct(queries.shape, jnp.bfloat16),
        grid_spec=pltpu.PrefetchScalarGridSpec(
            num_scalar_prefetch=1,
            grid=(width // cols,),
            in_specs=[
                pl.BlockSpec(rows.shape, lambda i, place: (0, 0), pipeline_mode=pl.Buffered(1))
                for rows in (*blocks, *before)
            ]
            + [pl.BlockSpec(memory_space=pltpu.VMEM) if kept else pl.BlockSpec((1, depth, cols), column)] * 2
            + [pl.BlockSpec((1, tokens, cols), column)]
            + [
                pl.BlockSpec((heads, *rows.shape[1:]), lambda i, place: (i, 0, 0, 0))
                for rows in kept
            ],
            out_specs=pl.BlockSpec((1, tokens, cols), column),
            scratch_shapes=[
                pltpu.VMEM((total + halo, depth), jnp.bfloat16),
                late,
                late,
                past,
                past,
            ],
        ),
        compiler_params=pltpu.CompilerParams(
            dimension_semantics=("arbitrary",), vmem_limit_bytes=VMEM_LIMIT
        ),
        name="attend",
    )(place, *blocks, *before, key_weight, value_weight, queries, *kept)


def swap(rows, axes, sizes, move):
    pairs = []
    for phase in range(sizes[0]):
        for part in range(sizes[1]):
            to = move(phase, part)
            pairs.append((phase * sizes[1] + part, to[0] * sizes[1] + to[1]))
    return lax.ppermute(rows, axes, pairs)


def on_device_staged(place, block, tail, ahead, sizes, key_weight, value_weight, queries):
    axes = ("phase", "mp")
    core = lambda rows: swap(rows, axes, sizes, lambda p, m: (p ^ 1, m))
    x_even = lambda rows: swap(
        rows, axes, sizes, lambda p, m: (p ^ 2, m) if p % 2 == 0 else (p, m ^ 1)
    )
    y_even = lambda rows: swap(
        rows, axes, sizes, lambda p, m: (p ^ 2, m) if p % 2 else (p, m ^ 1)
    )
    segs = queries.shape[1] // SEGLEN

    over_a = y_even(block)
    over_b = x_even(block)
    beside = core(block)
    passed = lax.ppermute(tail, "seq", ahead)
    carried = project([block, beside], key_weight, value_weight, 0, 4, segs)
    corner = x_even(over_a)
    beside_a = core(over_a)
    beside_b = core(over_b)
    passed = jnp.concatenate([passed, y_even(passed)], axis=0)
    carried = project([over_a, over_b], key_weight, value_weight, 1, 4, segs, carried)
    passed = jnp.concatenate([passed, x_even(passed)], axis=0)
    before = core(passed)
    beside_corner = core(corner)
    carried = project([beside_a, beside_b], key_weight, value_weight, 2, 4, segs, carried)
    carried = project([corner, beside_corner], key_weight, value_weight, 3, 4, segs, carried)
    before = [passed, before]
    return attend(place, [], before, key_weight, value_weight, queries, carried)


def attention(queries, key_weight, value_weight, enc_gain, neighbour_states, slot_dest):
    shards = lax.axis_size("seq")
    sizes = (lax.axis_size("phase"), lax.axis_size("mp"))
    own = lax.axis_index("seq")
    tokens_here = queries.shape[1]
    per_shard = NEIGH * (tokens_here // SEGLEN)
    capacity = per_shard // shards + 1
    _, tall, depth = neighbour_states.shape
    ahead = [(i, i + 1) for i in range(shards - 1)]
    even = lax.axis_index("phase") & 1 ^ 1
    place = jnp.stack([own, jnp.where(own == 0, 1, 0), even]).astype(jnp.int32)
    if sizes == (4, 2) and tall % TILE == 0 and capacity * tall <= LANES:
        parcels = pack(
            slot_dest,
            place,
            neighbour_states,
            enc_gain,
            shards,
            per_shard,
            capacity,
        )
        key_weight, value_weight = hold(key_weight, value_weight)
        arrived = [parcels[0]]
        for away in range(1, shards):
            pairs = [(i, (i + away) % shards) for i in range(shards)]
            arrived.append(lax.ppermute(parcels[away], "seq", pairs))
        block, tail = unpack(arrived, depth, per_shard, tall)
        return on_device_staged(
            place, block, tail, ahead, sizes, key_weight, value_weight, queries
        )
    normed = normalize(neighbour_states, enc_gain)
    block = route_plain(slot_dest, normed, own, shards, per_shard, capacity)
    before = lax.ppermute(block[per_shard - NEIGH :], "seq", ahead)
    block = jnp.concatenate([block, before], axis=0)
    routed = lax.all_gather(block, ("phase", "mp"), axis=1, tiled=True)
    mine, before = routed[:per_shard], routed[per_shard:]
    return attend(
        place,
        [mine.reshape(-1, depth)],
        [before.reshape(-1, depth)],
        key_weight,
        value_weight,
        queries,
    )


def solution(mesh):
    in_specs = (
        P("phase", "seq", "mp"),
        P("phase", None, "mp"),
        P("phase", None, "mp"),
        P(),
        P("seq", ("phase", "mp"), None),
        P("seq"),
    )
    out_specs = P("phase", "seq", "mp")
    return jax.shard_map(
        attention, mesh=mesh, in_specs=in_specs, out_specs=out_specs, check_vma=False
    )
```
